32 devices in a mesh: row: 8 (over y, x, core), col: 4 (over z).
Axes of the slice: x: 2, y: 2, z: 4, core: 2. Of those that a mesh axis runs over, the one named last changes fastest.
Arguments:
- contact_map: bfloat16 [512, 512, 128], P('row', 'col'), may hold values from -6 to 6
- conv_weight: bfloat16 [2, 3, 3, 3, 128, 128], replicated, may hold values from -0.1875 to 0.1875
- conv_bias: float32 [2, 3, 128], replicated, may hold values from -0.5 to 0.5
Outputs:
- trunk_out: bfloat16 [512, 512, 128], P('row', 'col')
The draws below stay inside these ranges and needn't reach their ends.
All inputs are finite; a program needn't handle non-finite values.
Results may differ from the reference program's by a relative error of at most 0.0085.
Values may be sent and summed in bfloat16 or wider, within the bound.
A program may use at most 128 MiB of HBM per device.

```python
import jax
import jax.numpy as jnp
from jax import lax

CH = 128
BLOCKS = 2
BINS = 512


def levels(rng, extent, split, smallest, top_value):
    level, own = 1.0, jax.random.fold_in(rng, 6)
    for position, parts in split:
        heights = jnp.exp(jax.random.uniform(jax.random.fold_in(own, position), (parts,), jnp.float32, smallest / len(split), top_value / len(split)))
        level = level * jnp.repeat(heights, extent[position] // parts).reshape([-1 if axis == position else 1 for axis in range(len(extent))])
    return level


def gaussian(key, dims, spread, bound, cuts=(), held_as=jnp.bfloat16):
    values = jax.random.normal(key, dims, jnp.float32) * spread
    if len(cuts) > 0:
        values = levels(key, dims, cuts, -0.22, 0.18) * values
    return jnp.clip(values, min=-bound, max=bound).astype(held_as)


def setup_inputs(seed: int = 0) -> dict:
    streams_of = jax.random.split(jax.random.key(seed), 4)
    return {
        "contact_map": gaussian(streams_of[0], (BINS, BINS, CH), 1.0, 6.0, ((0, 8), (1, 4))),
        "conv_weight": gaussian(streams_of[1], (BLOCKS, 3, 3, 3, CH, CH), (9 * CH) ** -0.5, 0.1875),
        "conv_bias": jnp.clip(jax.random.uniform(streams_of[2], (BLOCKS, 3, CH), jnp.float32, -0.5, 0.5), -0.5, 0.5),
    }


def convolve(field, kernel, dilation):
    result = lax.conv_general_dilated(field[None], kernel.astype(jnp.float32), (1, 1), [(dilation, dilation), (dilation, dilation)], rhs_dilation=(dilation, dilation), dimension_numbers=("NHWC", "HWIO", "NHWC"), precision=lax.Precision.HIGHEST)
    return result[0]


def reference(contact_map, conv_weight, conv_bias):
    current = contact_map
    for block in range(BLOCKS):
        mirrored = ((current.astype(jnp.float32) + jnp.transpose(current, (1, 0, 2)).astype(jnp.float32)) * 0.5).astype(jnp.bfloat16)
        hidden = mirrored
        for layer, dilation in enumerate((1, 2, 4)):
            total = convolve(hidden.astype(jnp.float32), conv_weight[block, layer], dilation) + conv_bias[block, layer]
            if layer < 2:
                hidden = jax.nn.relu(total).astype(jnp.bfloat16)
            else:
                current = (mirrored.astype(jnp.float32) + total).astype(jnp.bfloat16)
    return current
```

```python
import functools

import jax
import jax.numpy as jnp
from jax import lax
from jax.experimental import pallas as pl
from jax.experimental.pallas import tpu as pltpu
from jax.sharding import PartitionSpec as P

BF16, F32 = jnp.bfloat16, jnp.float32
DILATIONS = (1, 2, 4)
ROW_HALO = 2 * sum(DILATIONS)
COL_HALO = 16


def pair_weights(w):
    c = w.shape[2]
    a0, a1, a2 = (w[a].reshape(3 * c, c) for a in range(3))
    zero = jnp.zeros_like(a0)
    left = jnp.concatenate([a0, a1, a2, zero], axis=0)
    right = jnp.concatenate([zero, a0, a1, a2], axis=0)
    return jnp.concatenate([left, right], axis=1)


def trunk_kernel(rows, cols, where_ref, map_ref, both_ref, wide_ref, bias_ref, out_ref,
                 buf_a, buf_b, buf_c, cur_ref, mir_ref):
    tall, wide, ch = map_ref.shape
    row0, col0, bins = where_ref[0], where_ref[1], where_ref[2]
    position = lax.broadcasted_iota(jnp.int32, (wide, ch), 0) + (col0 - COL_HALO)
    col_ok = (position >= 0) & (position < bins)

    def keep(value, row):
        place = row0 - ROW_HALO + row
        inside = (place >= 0) & (place < bins)
        return jnp.where(col_ok & inside, value, 0.0)

    def spread(dst, row, value, d):
        dst[row, :, 0:ch] = pltpu.roll(value, d, 0).astype(BF16)
        dst[row, :, ch:2 * ch] = value.astype(BF16)
        dst[row, :, 2 * ch:3 * ch] = pltpu.roll(value, wide - d, 0).astype(BF16)

    def pairs(src, weight, d, first, last, emit, cut=slice(None)):
        count = min(d, 2)
        steps = (last - first) // (2 * count)

        @pl.loop(0, steps)
        def _(step):
            if d == 4:
                r = first + (step // 2) * 8 + (step % 2) * 2
            else:
                r = first + step * 2 * count
            taps = [src[pl.ds(r + k * d, count), cut, :] for k in (-1, 0, 1, 2)]
            lhs = jnp.concatenate([t.reshape(-1, 3 * ch) for t in taps], axis=1)
            total = jnp.dot(lhs, wide_ref[weight], preferred_element_type=F32)
            n = total.shape[0] // count
            for k in range(count):
                emit(r + k, total[k * n:(k + 1) * n, :ch])
                emit(r + k + d, total[k * n:(k + 1) * n, ch:])

    def relu_into(dst, bias, d):
        def emit(row, total):
            value = jnp.maximum(total + bias_ref[bias], 0.0)
            spread(dst, row, keep(value, row), d)
        return emit

    @pl.loop(0, tall)
    def _(row):
        spread(buf_a, row, map_ref[row].astype(F32), 1)

    @pl.loop(1, tall - 1)
    def _(row):
        lhs = jnp.concatenate([buf_a[row - 1], buf_a[row], buf_a[row + 1]], axis=1)
        total = jnp.dot(lhs, both_ref[...], preferred_element_type=F32)
        relu_into(buf_b, 0, 2)(row, total[:, :ch])
        relu_into(buf_c, 0, 2)(row, total[:, ch:])

    def first_out(row, total):
        cur_ref[row] = (map_ref[row].astype(F32) + total + bias_ref[2]).astype(BF16)

    def second_out(row, total):
        other = (map_ref[row].astype(F32) + total + bias_ref[2]).astype(BF16)
        value = ((cur_ref[row].astype(F32) + other.astype(F32)) * 0.5).astype(BF16)
        value = keep(value.astype(F32), row)
        mir_ref[row] = value.astype(BF16)
        spread(buf_b, row, value, 1)

    pairs(buf_b, 0, 2, 2, tall - 2, relu_into(buf_a, 1, 4))
    pairs(buf_a, 1, 4, 6, tall - 6, first_out)
    pairs(buf_c, 2, 2, 2, tall - 2, relu_into(buf_a, 1, 4))
    pairs(buf_a, 3, 4, 6, tall - 6, second_out)

    pairs(buf_b, 4, 1, 8, tall - 8, relu_into(buf_c, 3, 2))
    pairs(buf_c, 5, 2, 10, tall - 10, relu_into(buf_a, 4, 4))

    mid = slice(COL_HALO, COL_HALO + cols)

    def last_out(row, total):
        value = mir_ref[row, mid, :].astype(F32) + total + bias_ref[5]
        out_ref[row - ROW_HALO] = value.astype(BF16)

    pairs(buf_a, 6, 4, ROW_HALO, ROW_HALO + rows, last_out, mid)


def trunk(padded, where, conv_weight, conv_bias, rows, cols):
    tall, wide, ch = padded.shape
    flip = jnp.swapaxes(conv_weight[0], 1, 2)
    both = jnp.concatenate(
        [conv_weight[0, 0].reshape(9 * ch, ch), flip[0].reshape(9 * ch, ch)], axis=1)
    wides = jnp.stack([pair_weights(w) for w in (
        conv_weight[0, 1], conv_weight[0, 2], flip[1], flip[2],
        conv_weight[1, 0], conv_weight[1, 1], conv_weight[1, 2])])
    vmem = pl.BlockSpec(memory_space=pltpu.VMEM)
    return pl.pallas_call(
        functools.partial(trunk_kernel, rows, cols),
        out_shape=jax.ShapeDtypeStruct((rows, cols, ch), BF16),
        in_specs=[pl.BlockSpec(memory_space=pltpu.SMEM)] + [vmem] * 4,
        out_specs=vmem,
        scratch_shapes=[pltpu.VMEM((tall, wide, 3 * ch), BF16)] * 3
        + [pltpu.VMEM((tall, wide, ch), BF16)] * 2,
        compiler_params=pltpu.CompilerParams(vmem_limit_bytes=60 * 1024 * 1024),
    )(where, padded, both, wides, conv_bias.reshape(6, 1, ch))


def mirror(mine):
    half = mine.shape[0]
    n_row, n_col = lax.axis_size("row"), lax.axis_size("col")
    core = lax.axis_index("row") % 2
    parts = []
    for turn in range(2):
        side = (core + turn) % 2
        piece = lax.dynamic_slice_in_dim(mine, side * half, half, axis=1)
        route = []
        for r in range(n_row):
            for c in range(n_col):
                target = (2 * c + (r + turn) % 2) * n_col + r // 2
                route.append((r * n_col + c, target))
        got = lax.ppermute(piece, ("row", "col"), route)
        parts.append(jnp.swapaxes(got, 0, 1))
    low = jnp.where(core == 0, parts[0], parts[1])
    high = jnp.where(core == 0, parts[1], parts[0])
    flipped = jnp.concatenate([low, high], axis=1)
    return ((mine.astype(F32) + flipped.astype(F32)) * 0.5).astype(BF16)


def with_halo(array, axis, dim, width):
    devices, length = lax.axis_size(axis), array.shape[dim]
    up = [(i, i + 1) for i in range(devices - 1)]
    down = [(j, i) for i, j in up]
    before = lax.ppermute(lax.slice_in_dim(array, length - width, length, axis=dim), axis, up)
    after = lax.ppermute(lax.slice_in_dim(array, 0, width, axis=dim), axis, down)
    return jnp.concatenate([before, array, after], axis=dim)


def per_device(contact_map, conv_weight, conv_bias):
    rows, cols, _ = contact_map.shape
    mirrored = mirror(contact_map)
    padded = with_halo(mirrored, "row", 0, ROW_HALO)
    padded = with_halo(padded, "col", 1, COL_HALO)
    where = jnp.stack([
        lax.axis_index("row") * rows, lax.axis_index("col") * cols, lax.axis_size("row") * rows,
    ]).astype(jnp.int32)
    return trunk(padded, where, conv_weight, conv_bias, rows, cols)


def solution(mesh):
    in_specs = (P("row", "col", None), P(), P())
    out_specs = P("row", "col", None)
    return jax.shard_map(
        per_device, mesh=mesh, in_specs=in_specs, out_specs=out_specs, check_vma=False
    )
```

```python
import functools

import jax
import jax.numpy as jnp
from jax import lax
from jax.experimental import pallas as pl
from jax.experimental.pallas import tpu as pltpu
from jax.sharding import PartitionSpec as P

BF16, F32 = jnp.bfloat16, jnp.float32
DILATIONS = (1, 2, 4)
ROW_HALO = 2 * sum(DILATIONS)
COL_HALO = 16
CHUNKS = 8
MESH = pl.DeviceIdType.MESH


def pair_weights(w):
    c = w.shape[2]
    a0, a1, a2 = (w[a].reshape(3 * c, c) for a in range(3))
    zero = jnp.zeros_like(a0)
    left = jnp.concatenate([a0, a1, a2, zero], axis=0)
    right = jnp.concatenate([zero, a0, a1, a2], axis=0)
    return jnp.concatenate([left, right], axis=1)


def trunk_kernel(rows, cols, where_ref, map_ref, both_ref, wide_ref, bias_ref, out_ref,
                 buf_a, buf_b, buf_c, cur_ref, mir_ref):
    tall, wide, ch = map_ref.shape
    row0, col0, bins = where_ref[0], where_ref[1], where_ref[2]
    position = lax.broadcasted_iota(jnp.int32, (wide, ch), 0) + (col0 - COL_HALO)
    col_ok = (position >= 0) & (position < bins)

    def keep(value, row):
        place = row0 - ROW_HALO + row
        inside = (place >= 0) & (place < bins)
        return jnp.where(col_ok & inside, value, 0.0)

    def spread(dst, row, value, d):
        dst[row, :, 0:ch] = pltpu.roll(value, d, 0).astype(BF16)
        dst[row, :, ch:2 * ch] = value.astype(BF16)
        dst[row, :, 2 * ch:3 * ch] = pltpu.roll(value, wide - d, 0).astype(BF16)

    def pairs(src, weight, d, first, last, emit, cut=slice(None)):
        count = min(d, 2)
        steps = (last - first) // (2 * count)

        @pl.loop(0, steps)
        def _(step):
            if d == 4:
                r = first + (step // 2) * 8 + (step % 2) * 2
            else:
                r = first + step * 2 * count
            taps = [src[pl.ds(r + k * d, count), cut, :] for k in (-1, 0, 1, 2)]
            lhs = jnp.concatenate([t.reshape(-1, 3 * ch) for t in taps], axis=1)
            total = jnp.dot(lhs, wide_ref[weight], preferred_element_type=F32)
            n = total.shape[0] // count
            for k in range(count):
                emit(r + k, total[k * n:(k + 1) * n, :ch])
                emit(r + k + d, total[k * n:(k + 1) * n, ch:])

    def relu_into(dst, bias, d):
        def emit(row, total):
            value = jnp.maximum(total + bias_ref[bias], 0.0)
            spread(dst, row, keep(value, row), d)
        return emit

    @pl.loop(0, tall)
    def _(row):
        spread(buf_a, row, map_ref[row].astype(F32), 1)

    @pl.loop(1, tall - 1)
    def _(row):
        lhs = jnp.concatenate([buf_a[row - 1], buf_a[row], buf_a[row + 1]], axis=1)
        total = jnp.dot(lhs, both_ref[...], preferred_element_type=F32)
        relu_into(buf_b, 0, 2)(row, total[:, :ch])
        relu_into(buf_c, 0, 2)(row, total[:, ch:])

    def first_out(row, total):
        cur_ref[row] = (map_ref[row].astype(F32) + total + bias_ref[2]).astype(BF16)

    def second_out(row, total):
        other = (map_ref[row].astype(F32) + total + bias_ref[2]).astype(BF16)
        value = ((cur_ref[row].astype(F32) + other.astype(F32)) * 0.5).astype(BF16)
        value = keep(value.astype(F32), row)
        mir_ref[row] = value.astype(BF16)
        spread(buf_b, row, value, 1)

    pairs(buf_b, 0, 2, 2, tall - 2, relu_into(buf_a, 1, 4))
    pairs(buf_a, 1, 4, 6, tall - 6, first_out)
    pairs(buf_c, 2, 2, 2, tall - 2, relu_into(buf_a, 1, 4))
    pairs(buf_a, 3, 4, 6, tall - 6, second_out)

    pairs(buf_b, 4, 1, 8, tall - 8, relu_into(buf_c, 3, 2))
    pairs(buf_c, 5, 2, 10, tall - 10, relu_into(buf_a, 4, 4))

    mid = slice(COL_HALO, COL_HALO + cols)

    def last_out(row, total):
        value = mir_ref[row, mid, :].astype(F32) + total + bias_ref[5]
        out_ref[row - ROW_HALO] = value.astype(BF16)

    pairs(buf_a, 6, 4, ROW_HALO, ROW_HALO + rows, last_out, mid)


def trunk(padded, where, conv_weight, conv_bias, rows, cols):
    tall, wide, ch = padded.shape
    flip = jnp.swapaxes(conv_weight[0], 1, 2)
    both = jnp.concatenate(
        [conv_weight[0, 0].reshape(9 * ch, ch), flip[0].reshape(9 * ch, ch)], axis=1)
    wides = jnp.stack([pair_weights(w) for w in (
        conv_weight[0, 1], conv_weight[0, 2], flip[1], flip[2],
        conv_weight[1, 0], conv_weight[1, 1], conv_weight[1, 2])])
    vmem = pl.BlockSpec(memory_space=pltpu.VMEM)
    return pl.pallas_call(
        functools.partial(trunk_kernel, rows, cols),
        out_shape=jax.ShapeDtypeStruct((rows, cols, ch), BF16),
        in_specs=[pl.BlockSpec(memory_space=pltpu.SMEM)] + [vmem] * 4,
        out_specs=vmem,
        scratch_shapes=[pltpu.VMEM((tall, wide, 3 * ch), BF16)] * 3
        + [pltpu.VMEM((tall, wide, ch), BF16)] * 2,
        compiler_params=pltpu.CompilerParams(vmem_limit_bytes=60 * 1024 * 1024),
    )(where, padded, both, wides, conv_bias.reshape(6, 1, ch))


def exchange_kernel(via_source, n_col, map_ref, out_ref, stage_ref,
                    send_sem, recv_sem, stage_sem, pass_sem, own_sem):
    row, col = lax.axis_index("row"), lax.axis_index("col")
    a, e, b = row // 2, row % 2, col
    half = map_ref.shape[0]
    size = half // CHUNKS
    diagonal = a == b

    def relayed(source, target, k):
        inner_source = (source > 0) & (source < n_col - 1)
        inner_target = (target > 0) & (target < n_col - 1)
        gap = source - target
        near = ((gap == 1) | (gap == -1)) & (inner_source != inner_target)
        inner = inner_source if via_source else inner_target
        most, some, few = k % 4 != 0, k % 2 == 1, k % 4 == 3
        share = jnp.where(near, jnp.where(inner, most, few), some)
        return (source != target) & share

    def piece(k, f):
        return map_ref.at[pl.ds(k * size, size), pl.ds(f * half, half), :]

    def land(core, k):
        return out_ref.at[core, pl.ds(k * size, size)]

    def signal(r, c):
        pl.semaphore_signal(barrier, inc=1, device_id=(r, c), device_id_type=MESH)

    barrier = pltpu.get_barrier_semaphore()

    @pl.when(jnp.logical_not(diagonal))
    def _():
        for f in range(2):
            signal(2 * b + f, a)
            signal(2 * b + f, b)
        signal(2 * a + e, a)
        pl.semaphore_wait(barrier, 5)

    @pl.when(diagonal)
    def _():
        signal(2 * a + 1 - e, a)
        for s in range(1, n_col):
            other = lax.rem(a + s, n_col)
            if via_source:
                signal(2 * a + e, other)
                signal(2 * other, a)
                signal(2 * other + 1, a)
            else:
                signal(2 * other, a)
                signal(2 * other + 1, a)
                signal(2 * a + e, other)
        pl.semaphore_wait(barrier, 3 * (n_col - 1) + 1)

    def direct(k, f):
        return pltpu.make_async_remote_copy(
            src_ref=piece(k, f), dst_ref=land(e, k), send_sem=send_sem.at[f, k],
            recv_sem=recv_sem.at[e, k], device_id=(2 * b + f, a), device_id_type=MESH)

    def first_hop(k, f):
        if via_source:
            slot, place = (b, f, k), (2 * a + e, a)
        else:
            slot, place = (a, e, k), (2 * b + f, b)
        return pltpu.make_async_remote_copy(
            src_ref=piece(k, f), dst_ref=stage_ref.at[slot], send_sem=send_sem.at[f, k],
            recv_sem=stage_sem.at[slot], device_id=place, device_id_type=MESH)

    def second_hop(k, other, bit):
        if via_source:
            core, place = e, (2 * other + bit, a)
        else:
            core, place = bit, (2 * a + e, other)
        return pltpu.make_async_remote_copy(
            src_ref=stage_ref.at[other, bit, k], dst_ref=land(core, k),
            send_sem=pass_sem.at[other, bit, k], recv_sem=recv_sem.at[core, k],
            device_id=place, device_id_type=MESH)

    def own(k):
        return pltpu.make_async_copy(piece(k, e), land(e, k), own_sem.at[k])

    order = [k for k in range(CHUNKS) if k % 2] + [k for k in range(CHUNKS) if k % 2 == 0]

    @pl.when(jnp.logical_not(diagonal))
    def _():
        for k in order:
            for f in range(2):
                through = relayed(a, b, k)

                @pl.when(through)
                def _():
                    first_hop(k, f).start()

                @pl.when(jnp.logical_not(through))
                def _():
                    direct(k, f).start()

        for k in range(CHUNKS):
            for f in range(2):
                direct(k, f).wait_send()
                pltpu.make_async_remote_copy(
                    src_ref=land(f, k), dst_ref=land(f, k), send_sem=send_sem.at[f, k],
                    recv_sem=recv_sem.at[f, k], device_id=(2 * b + f, a),
                    device_id_type=MESH).wait_recv()

    def cross(k):
        return pltpu.make_async_remote_copy(
            src_ref=piece(k, 1 - e), dst_ref=land(e, k), send_sem=send_sem.at[0, k],
            recv_sem=recv_sem.at[e, k], device_id=(2 * a + 1 - e, a), device_id_type=MESH)

    def crossed(k):
        return pltpu.make_async_remote_copy(
            src_ref=land(1 - e, k), dst_ref=land(1 - e, k), send_sem=send_sem.at[0, k],
            recv_sem=recv_sem.at[1 - e, k], device_id=(2 * a + 1 - e, a), device_id_type=MESH)

    @pl.when(diagonal)
    def _():
        for k in range(CHUNKS):
            cross(k).start()
            own(k).start()

        def hops(act):
            for k in order:
                for s in range(1, n_col):
                    other = lax.rem(a + s, n_col)
                    source, target = (a, other) if via_source else (other, a)
                    for bit in range(2):
                        @pl.when(relayed(source, target, k))
                        def _():
                            act(second_hop(k, other, bit), k, other, bit)

        def forward(copy, k, other, bit):
            pltpu.make_async_remote_copy(
                src_ref=stage_ref.at[other, bit, k], dst_ref=stage_ref.at[other, bit, k],
                send_sem=pass_sem.at[other, bit, k], recv_sem=stage_sem.at[other, bit, k],
                device_id=(2 * a + 1 - e, a), device_id_type=MESH).wait_recv()
            copy.start()

        hops(forward)
        hops(lambda copy, k, other, bit: copy.wait_send())
        for k in range(CHUNKS):
            cross(k).wait_send()
            crossed(k).wait_recv()
            own(k).wait()


def exchange(mine, via_source=False):
    half, _, ch = mine.shape
    n_col = lax.axis_size("col")
    anywhere = pl.BlockSpec(memory_space=pl.ANY)
    out, _ = pl.pallas_call(
        functools.partial(exchange_kernel, via_source, n_col),
        out_shape=(jax.ShapeDtypeStruct((2, half, half, ch), BF16),
                   jax.ShapeDtypeStruct((n_col, 2, CHUNKS, half // CHUNKS, half, ch), BF16)),
        in_specs=[anywhere], out_specs=(anywhere, anywhere),
        scratch_shapes=[
            pltpu.SemaphoreType.DMA((2, CHUNKS)), pltpu.SemaphoreType.DMA((2, CHUNKS)),
            pltpu.SemaphoreType.DMA((n_col, 2, CHUNKS)), pltpu.SemaphoreType.DMA((n_col, 2, CHUNKS)),
            pltpu.SemaphoreType.DMA((CHUNKS,))],
        compiler_params=pltpu.CompilerParams(collective_id=0, has_side_effects=True),
    )(mine)
    return out


def mirror(mine):
    half, full, ch = mine.shape
    flipped = jnp.swapaxes(exchange(mine).reshape(full, half, ch), 0, 1)
    return ((mine.astype(F32) + flipped.astype(F32)) * 0.5).astype(BF16)


def with_halo(array, axis, dim, width):
    devices, length = lax.axis_size(axis), array.shape[dim]
    up = [(i, i + 1) for i in range(devices - 1)]
    down = [(j, i) for i, j in up]
    before = lax.ppermute(lax.slice_in_dim(array, length - width, length, axis=dim), axis, up)
    after = lax.ppermute(lax.slice_in_dim(array, 0, width, axis=dim), axis, down)
    return jnp.concatenate([before, array, after], axis=dim)


def per_device(contact_map, conv_weight, conv_bias):
    rows, cols, _ = contact_map.shape
    mirrored = mirror(contact_map)
    padded = with_halo(mirrored, "row", 0, ROW_HALO)
    padded = with_halo(padded, "col", 1, COL_HALO)
    where = jnp.stack([
        lax.axis_index("row") * rows, lax.axis_index("col") * cols, lax.axis_size("row") * rows,
    ]).astype(jnp.int32)
    return trunk(padded, where, conv_weight, conv_bias, rows, cols)


def solution(mesh):
    in_specs = (P("row", "col", None), P(), P())
    out_specs = P("row", "col", None)
    return jax.shard_map(
        per_device, mesh=mesh, in_specs=in_specs, out_specs=out_specs, check_vma=False
    )
```

```python
import functools

import jax
import jax.numpy as jnp
from jax import lax
from jax.experimental import pallas as pl
from jax.experimental.pallas import tpu as pltpu
from jax.sharding import PartitionSpec as P

BF16, F32 = jnp.bfloat16, jnp.float32
DILATIONS = (1, 2, 4)
ROW_HALO = 2 * sum(DILATIONS)
COL_HALO = 16
FIRST, PAIRS = 5, 4
WIDE = ((1, False), (2, False), (1, True), (2, True), (3, False), (4, False), (5, False))
CHUNKS = 8
MESH = pl.DeviceIdType.MESH


def trunk_kernel(rows, cols, where_ref, left_ref, mid_ref, right_ref, weight_ref, bias_ref, out_ref,
                 buf_a, buf_b, buf_c, cur_ref, mir_ref, map_ref, both_ref, wide_ref):
    tall, wide, ch = map_ref.shape
    row0, col0, bins = where_ref[0], where_ref[1], where_ref[2]
    position = lax.broadcasted_iota(jnp.int32, (wide, ch), 0) + (col0 - COL_HALO)
    col_ok = (position >= 0) & (position < bins)

    def keep(value, row):
        place = row0 - ROW_HALO + row
        inside = (place >= 0) & (place < bins)
        return jnp.where(col_ok & inside, value, 0.0)

    def spread(dst, row, value, d):
        dst[row, :, 0:ch] = pltpu.roll(value, d, 0).astype(BF16)
        dst[row, :, ch:2 * ch] = value.astype(BF16)
        dst[row, :, 2 * ch:3 * ch] = pltpu.roll(value, wide - d, 0).astype(BF16)

    def pairs(src, weight, d, first, last, emit, count, cut=slice(None)):
        @pl.loop(0, (last - first) // (2 * count))
        def _(step):
            base = first + step * (2 * count)
            tops = [base + (i // d) * 2 * d + i % d for i in range(count)]
            lhs = jnp.concatenate([
                jnp.concatenate([src[r + k * d, cut, :] for k in (-1, 0, 1, 2)], axis=1)
                for r in tops], axis=0)
            total = jnp.dot(lhs, wide_ref[weight], preferred_element_type=F32)
            n = total.shape[0] // count
            for i, r in enumerate(tops):
                emit(r, total[i * n:(i + 1) * n, :ch])
                emit(r + d, total[i * n:(i + 1) * n, ch:])

    def relu_into(dst, bias, d):
        def emit(row, total):
            value = jnp.maximum(total + bias_ref[bias], 0.0)
            spread(dst, row, keep(value, row), d)
        return emit

    for slot, (layer, flip) in enumerate(WIDE):
        zero = jnp.zeros((3 * ch, ch), BF16)
        wide_ref[slot, 9 * ch:12 * ch, 0:ch] = zero
        wide_ref[slot, 0:3 * ch, ch:2 * ch] = zero
        for tap in range(9):
            block = weight_ref[layer * 9 + (tap % 3 * 3 + tap // 3 if flip else tap)]
            wide_ref[slot, tap * ch:(tap + 1) * ch, 0:ch] = block
            wide_ref[slot, (tap + 3) * ch:(tap + 4) * ch, ch:2 * ch] = block
    for tap in range(9):
        both_ref[tap * ch:(tap + 1) * ch, 0:ch] = weight_ref[tap]
        both_ref[tap * ch:(tap + 1) * ch, ch:2 * ch] = weight_ref[tap % 3 * 3 + tap // 3]

    @pl.loop(0, tall)
    def _(row):
        map_ref[row, 0:COL_HALO] = left_ref[row]
        map_ref[row, COL_HALO:COL_HALO + cols] = mid_ref[row]
        map_ref[row, COL_HALO + cols:wide] = right_ref[row]
        spread(buf_a, row, map_ref[row].astype(F32), 1)

    @pl.loop(0, (tall - 2) // FIRST)
    def _(step):
        rows_here = [1 + step * FIRST + i for i in range(FIRST)]
        lhs = jnp.concatenate([
            jnp.concatenate([buf_a[row + k] for k in (-1, 0, 1)], axis=1) for row in rows_here], axis=0)
        total = jnp.dot(lhs, both_ref[...], preferred_element_type=F32)
        for i, row in enumerate(rows_here):
            relu_into(buf_b, 0, 2)(row, total[i * wide:(i + 1) * wide, :ch])
            relu_into(buf_c, 0, 2)(row, total[i * wide:(i + 1) * wide, ch:])

    def first_out(row, total):
        cur_ref[row] = (map_ref[row].astype(F32) + total + bias_ref[2]).astype(BF16)

    def second_out(row, total):
        other = (map_ref[row].astype(F32) + total + bias_ref[2]).astype(BF16)
        value = ((cur_ref[row].astype(F32) + other.astype(F32)) * 0.5).astype(BF16)
        value = keep(value.astype(F32), row)
        mir_ref[row] = value.astype(BF16)
        spread(buf_b, row, value, 1)

    pairs(buf_b, 0, 2, 2, tall - 2, relu_into(buf_a, 1, 4), PAIRS)
    pairs(buf_a, 1, 4, 6, tall - 6, first_out, PAIRS)
    pairs(buf_c, 2, 2, 2, tall - 2, relu_into(buf_a, 1, 4), PAIRS)
    pairs(buf_a, 3, 4, 6, tall - 6, second_out, PAIRS)

    pairs(buf_b, 4, 1, 8, tall - 8, relu_into(buf_c, 3, 2), 2)
    pairs(buf_c, 5, 2, 10, tall - 10, relu_into(buf_a, 4, 4), PAIRS)

    mid = slice(COL_HALO, COL_HALO + cols)

    def last_out(row, total):
        value = mir_ref[row, mid, :].astype(F32) + total + bias_ref[5]
        out_ref[row - ROW_HALO] = value.astype(BF16)

    pairs(buf_a, 6, 4, ROW_HALO, ROW_HALO + rows, last_out, PAIRS, mid)


def trunk(pieces, where, conv_weight, conv_bias, rows, cols):
    tall, _, ch = pieces[1].shape
    wide = cols + 2 * COL_HALO
    vmem = pl.BlockSpec(memory_space=pltpu.VMEM)
    return pl.pallas_call(
        functools.partial(trunk_kernel, rows, cols),
        out_shape=jax.ShapeDtypeStruct((rows, cols, ch), BF16),
        in_specs=[pl.BlockSpec(memory_space=pltpu.SMEM)] + [vmem] * 5,
        out_specs=vmem,
        scratch_shapes=[pltpu.VMEM((tall, wide, 3 * ch), BF16)] * 3
        + [pltpu.VMEM((tall, wide, ch), BF16)] * 3
        + [pltpu.VMEM((9 * ch, 2 * ch), BF16), pltpu.VMEM((len(WIDE), 12 * ch, 2 * ch), BF16)],
        compiler_params=pltpu.CompilerParams(vmem_limit_bytes=62 * 1024 * 1024),
    )(where, *pieces, conv_weight.reshape(54, ch, ch), conv_bias.reshape(6, 1, ch))


def exchange_kernel(via_source, n_col, map_ref, out_ref, stage_ref,
                    send_sem, recv_sem, stage_sem, pass_sem, own_sem):
    row, col = lax.axis_index("row"), lax.axis_index("col")
    a, e, b = row // 2, row % 2, col
    half = map_ref.shape[0]
    size = half // CHUNKS
    diagonal = a == b

    def relayed(source, target, k):
        inner_source = (source > 0) & (source < n_col - 1)
        inner_target = (target > 0) & (target < n_col - 1)
        gap = source - target
        near = ((gap == 1) | (gap == -1)) & (inner_source != inner_target)
        inner = inner_source if via_source else inner_target
        share = jnp.where(near, inner, k % 2 == 1)
        return (source != target) & share

    def piece(k, f):
        return map_ref.at[pl.ds(k * size, size), pl.ds(f * half, half), :]

    def land(core, k):
        return out_ref.at[core, pl.ds(k * size, size)]

    def signal(r, c):
        pl.semaphore_signal(barrier, inc=1, device_id=(r, c), device_id_type=MESH)

    barrier = pltpu.get_barrier_semaphore()

    @pl.when(jnp.logical_not(diagonal))
    def _():
        for f in range(2):
            signal(2 * b + f, a)
            signal(2 * b + f, b)
        signal(2 * a + e, a)
        pl.semaphore_wait(barrier, 5)

    @pl.when(diagonal)
    def _():
        signal(2 * a + 1 - e, a)
        for s in range(1, n_col):
            other = lax.rem(a + s, n_col)
            if via_source:
                signal(2 * a + e, other)
                signal(2 * other, a)
                signal(2 * other + 1, a)
            else:
                signal(2 * other, a)
                signal(2 * other + 1, a)
                signal(2 * a + e, other)
        pl.semaphore_wait(barrier, 3 * (n_col - 1) + 1)

    def direct(k, f):
        return pltpu.make_async_remote_copy(
            src_ref=piece(k, f), dst_ref=land(e, k), send_sem=send_sem.at[f, k],
            recv_sem=recv_sem.at[e, k], device_id=(2 * b + f, a), device_id_type=MESH)

    def first_hop(k, f):
        if via_source:
            slot, place = (b, f, k), (2 * a + e, a)
        else:
            slot, place = (a, e, k), (2 * b + f, b)
        return pltpu.make_async_remote_copy(
            src_ref=piece(k, f), dst_ref=stage_ref.at[slot], send_sem=send_sem.at[f, k],
            recv_sem=stage_sem.at[slot], device_id=place, device_id_type=MESH)

    def second_hop(k, other, bit):
        if via_source:
            core, place = e, (2 * other + bit, a)
        else:
            core, place = bit, (2 * a + e, other)
        return pltpu.make_async_remote_copy(
            src_ref=stage_ref.at[other, bit, k], dst_ref=land(core, k),
            send_sem=pass_sem.at[other, bit, k], recv_sem=recv_sem.at[core, k],
            device_id=place, device_id_type=MESH)

    def own(k):
        return pltpu.make_async_copy(piece(k, e), land(e, k), own_sem.at[k])

    order = list(range(CHUNKS))

    @pl.when(jnp.logical_not(diagonal))
    def _():
        for k in order:
            for f in range(2):
                through = relayed(a, b, k)

                @pl.when(through)
                def _():
                    first_hop(k, f).start()

                @pl.when(jnp.logical_not(through))
                def _():
                    direct(k, f).start()

        for k in range(CHUNKS):
            for f in range(2):
                direct(k, f).wait_send()
                pltpu.make_async_remote_copy(
                    src_ref=land(f, k), dst_ref=land(f, k), send_sem=send_sem.at[f, k],
                    recv_sem=recv_sem.at[f, k], device_id=(2 * b + f, a),
                    device_id_type=MESH).wait_recv()

    def cross(k):
        return pltpu.make_async_remote_copy(
            src_ref=piece(k, 1 - e), dst_ref=land(e, k), send_sem=send_sem.at[0, k],
            recv_sem=recv_sem.at[e, k], device_id=(2 * a + 1 - e, a), device_id_type=MESH)

    def crossed(k):
        return pltpu.make_async_remote_copy(
            src_ref=land(1 - e, k), dst_ref=land(1 - e, k), send_sem=send_sem.at[0, k],
            recv_sem=recv_sem.at[1 - e, k], device_id=(2 * a + 1 - e, a), device_id_type=MESH)

    @pl.when(diagonal)
    def _():
        for k in range(CHUNKS):
            cross(k).start()
            own(k).start()

        def hops(act):
            for k in order:
                for s in range(1, n_col):
                    other = lax.rem(a + s, n_col)
                    source, target = (a, other) if via_source else (other, a)
                    for bit in range(2):
                        @pl.when(relayed(source, target, k))
                        def _():
                            act(second_hop(k, other, bit), k, other, bit)

        def forward(copy, k, other, bit):
            pltpu.make_async_remote_copy(
                src_ref=stage_ref.at[other, bit, k], dst_ref=stage_ref.at[other, bit, k],
                send_sem=pass_sem.at[other, bit, k], recv_sem=stage_sem.at[other, bit, k],
                device_id=(2 * a + 1 - e, a), device_id_type=MESH).wait_recv()
            copy.start()

        hops(forward)
        hops(lambda copy, k, other, bit: copy.wait_send())
        for k in range(CHUNKS):
            cross(k).wait_send()
            crossed(k).wait_recv()
            own(k).wait()


def exchange(mine, via_source=False):
    half, _, ch = mine.shape
    n_col = lax.axis_size("col")
    anywhere = pl.BlockSpec(memory_space=pl.ANY)
    out, _ = pl.pallas_call(
        functools.partial(exchange_kernel, via_source, n_col),
        out_shape=(jax.ShapeDtypeStruct((2, half, half, ch), BF16),
                   jax.ShapeDtypeStruct((n_col, 2, CHUNKS, half // CHUNKS, half, ch), BF16)),
        in_specs=[anywhere], out_specs=(anywhere, anywhere),
        scratch_shapes=[
            pltpu.SemaphoreType.DMA((2, CHUNKS)), pltpu.SemaphoreType.DMA((2, CHUNKS)),
            pltpu.SemaphoreType.DMA((n_col, 2, CHUNKS)), pltpu.SemaphoreType.DMA((n_col, 2, CHUNKS)),
            pltpu.SemaphoreType.DMA((CHUNKS,))],
        compiler_params=pltpu.CompilerParams(collective_id=0, has_side_effects=True),
    )(mine)
    return out


def mirror(mine):
    half, full, ch = mine.shape
    flipped = jnp.swapaxes(exchange(mine).reshape(full, half, ch), 0, 1)
    return ((mine.astype(F32) + flipped.astype(F32)) * 0.5).astype(BF16)


def halo(array, axis, dim, width):
    devices, length = lax.axis_size(axis), array.shape[dim]
    up = [(i, i + 1) for i in range(devices - 1)]
    down = [(j, i) for i, j in up]
    before = lax.ppermute(lax.slice_in_dim(array, length - width, length, axis=dim), axis, up)
    after = lax.ppermute(lax.slice_in_dim(array, 0, width, axis=dim), axis, down)
    return before, array, after


def per_device(contact_map, conv_weight, conv_bias):
    rows, cols, _ = contact_map.shape
    mirrored = mirror(contact_map)
    tall = jnp.concatenate(halo(mirrored, "row", 0, ROW_HALO), axis=0)
    pieces = halo(tall, "col", 1, COL_HALO)
    where = jnp.stack([
        lax.axis_index("row") * rows, lax.axis_index("col") * cols, lax.axis_size("row") * rows,
    ]).astype(jnp.int32)
    return trunk(pieces, where, conv_weight, conv_bias, rows, cols)


def solution(mesh):
    in_specs = (P("row", "col", None), P(), P())
    out_specs = P("row", "col", None)
    return jax.shard_map(
        per_device, mesh=mesh, in_specs=in_specs, out_specs=out_specs, check_vma=False
    )
```

```python
import functools

import jax
import jax.numpy as jnp
from jax import lax
from jax.experimental import pallas as pl
from jax.experimental.pallas import tpu as pltpu
from jax.sharding import PartitionSpec as P

BF16, F32 = jnp.bfloat16, jnp.float32
DILATIONS = (1, 2, 4)
ROW_HALO = 2 * sum(DILATIONS)
COL_HALO = 16
FIRST, PAIRS = 10, 4
WIDE = ((1, False), (2, False), (1, True), (2, True), (3, False), (4, False), (5, False))
CHUNKS = 16
MESH = pl.DeviceIdType.MESH


def trunk_kernel(rows, cols, where_ref, left_ref, mid_ref, right_ref, weight_ref, bias_ref, out_ref,
                 buf_a, buf_b, buf_c, cur_ref, mir_ref, map_ref, both_ref, wide_ref):
    tall, wide, ch = map_ref.shape
    row0, col0, bins = where_ref[0], where_ref[1], where_ref[2]
    position = lax.broadcasted_iota(jnp.int32, (wide, ch), 0) + (col0 - COL_HALO)
    col_ok = (position >= 0) & (position < bins)

    def keep(value, row):
        place = row0 - ROW_HALO + row
        inside = (place >= 0) & (place < bins)
        return jnp.where(col_ok & inside, value, 0.0)

    def spread(dst, row, value, d):
        dst[row, :, 0:ch] = pltpu.roll(value, d, 0).astype(BF16)
        dst[row, :, ch:2 * ch] = value.astype(BF16)
        dst[row, :, 2 * ch:3 * ch] = pltpu.roll(value, wide - d, 0).astype(BF16)

    def pairs(src, weight, d, first, last, emit, count, cut=slice(None)):
        @pl.loop(0, (last - first) // (2 * count))
        def _(step):
            base = first + step * (2 * count)
            tops = [base + (i // d) * 2 * d + i % d for i in range(count)]
            lhs = jnp.concatenate([
                jnp.concatenate([src[r + k * d, cut, :] for k in (-1, 0, 1, 2)], axis=1)
                for r in tops], axis=0)
            total = jnp.dot(lhs, wide_ref[weight], preferred_element_type=F32)
            n = total.shape[0] // count
            for i, r in enumerate(tops):
                emit(r, total[i * n:(i + 1) * n, :ch])
                emit(r + d, total[i * n:(i + 1) * n, ch:])

    def relu_into(dst, bias, d):
        def emit(row, total):
            value = jnp.maximum(total + bias_ref[bias], 0.0)
            spread(dst, row, keep(value, row), d)
        return emit

    for slot, (layer, flip) in enumerate(WIDE):
        zero = jnp.zeros((3 * ch, ch), BF16)
        wide_ref[slot, 9 * ch:12 * ch, 0:ch] = zero
        wide_ref[slot, 0:3 * ch, ch:2 * ch] = zero
        for tap in range(9):
            block = weight_ref[layer * 9 + (tap % 3 * 3 + tap // 3 if flip else tap)]
            wide_ref[slot, tap * ch:(tap + 1) * ch, 0:ch] = block
            wide_ref[slot, (tap + 3) * ch:(tap + 4) * ch, ch:2 * ch] = block
    for tap in range(9):
        both_ref[tap * ch:(tap + 1) * ch, 0:ch] = weight_ref[tap]
        both_ref[tap * ch:(tap + 1) * ch, ch:2 * ch] = weight_ref[tap % 3 * 3 + tap // 3]

    @pl.loop(0, tall)
    def _(row):
        map_ref[row, 0:COL_HALO] = left_ref[row]
        map_ref[row, COL_HALO:COL_HALO + cols] = mid_ref[row]
        map_ref[row, COL_HALO + cols:wide] = right_ref[row]
        spread(buf_a, row, map_ref[row].astype(F32), 1)

    @pl.loop(0, (tall - 2) // FIRST)
    def _(step):
        rows_here = [1 + step * FIRST + i for i in range(FIRST)]
        lhs = jnp.concatenate([
            jnp.concatenate([buf_a[row + k] for k in (-1, 0, 1)], axis=1) for row in rows_here], axis=0)
        total = jnp.dot(lhs, both_ref[...], preferred_element_type=F32)
        for i, row in enumerate(rows_here):
            relu_into(buf_b, 0, 2)(row, total[i * wide:(i + 1) * wide, :ch])
            relu_into(buf_c, 0, 2)(row, total[i * wide:(i + 1) * wide, ch:])

    def first_out(row, total):
        cur_ref[row] = (map_ref[row].astype(F32) + total + bias_ref[2]).astype(BF16)

    def second_out(row, total):
        other = (map_ref[row].astype(F32) + total + bias_ref[2]).astype(BF16)
        value = ((cur_ref[row].astype(F32) + other.astype(F32)) * 0.5).astype(BF16)
        value = keep(value.astype(F32), row)
        mir_ref[row] = value.astype(BF16)
        spread(buf_b, row, value, 1)

    pairs(buf_b, 0, 2, 2, tall - 2, relu_into(buf_a, 1, 4), PAIRS)
    pairs(buf_a, 1, 4, 6, tall - 6, first_out, 8)
    pairs(buf_c, 2, 2, 2, tall - 2, relu_into(buf_a, 1, 4), PAIRS)
    pairs(buf_a, 3, 4, 6, tall - 6, second_out, 8)

    pairs(buf_b, 4, 1, 6, tall - 6, relu_into(buf_c, 3, 2), PAIRS)
    pairs(buf_c, 5, 2, 10, tall - 10, relu_into(buf_a, 4, 4), PAIRS)

    mid = slice(COL_HALO, COL_HALO + cols)

    def last_out(row, total):
        value = mir_ref[row, mid, :].astype(F32) + total + bias_ref[5]
        out_ref[row - ROW_HALO] = value.astype(BF16)

    pairs(buf_a, 6, 4, ROW_HALO, ROW_HALO + rows, last_out, 8, mid)


def trunk(pieces, where, conv_weight, conv_bias, rows, cols):
    tall, _, ch = pieces[1].shape
    wide = cols + 2 * COL_HALO
    vmem = pl.BlockSpec(memory_space=pltpu.VMEM)
    return pl.pallas_call(
        functools.partial(trunk_kernel, rows, cols),
        out_shape=jax.ShapeDtypeStruct((rows, cols, ch), BF16),
        in_specs=[pl.BlockSpec(memory_space=pltpu.SMEM)] + [vmem] * 5,
        out_specs=vmem,
        scratch_shapes=[pltpu.VMEM((tall, wide, 3 * ch), BF16)] * 3
        + [pltpu.VMEM((tall, wide, ch), BF16)] * 3
        + [pltpu.VMEM((9 * ch, 2 * ch), BF16), pltpu.VMEM((len(WIDE), 12 * ch, 2 * ch), BF16)],
        compiler_params=pltpu.CompilerParams(vmem_limit_bytes=62 * 1024 * 1024),
    )(where, *pieces, conv_weight.reshape(54, ch, ch), conv_bias.reshape(6, 1, ch))


def exchange_kernel(via_source, n_col, map_ref, out_ref, stage_ref,
                    send_sem, recv_sem, stage_sem, pass_sem, own_sem):
    row, col = lax.axis_index("row"), lax.axis_index("col")
    a, e, b = row // 2, row % 2, col
    half = map_ref.shape[0]
    size = half // CHUNKS
    diagonal = a == b

    def relayed(source, target, k):
        inner_source = (source > 0) & (source < n_col - 1)
        inner_target = (target > 0) & (target < n_col - 1)
        gap = source - target
        near = ((gap == 1) | (gap == -1)) & (inner_source != inner_target)
        inner = inner_source if via_source else inner_target
        share = jnp.where(near, jnp.where(inner, k % 8 != 0, k % 8 == 7), k % 16 in (1, 3, 5, 7, 9, 11, 13))
        return (source != target) & share

    def piece(k, f):
        return map_ref.at[pl.ds(k * size, size), pl.ds(f * half, half), :]

    def land(core, k):
        return out_ref.at[core, pl.ds(k * size, size)]

    def signal(r, c):
        pl.semaphore_signal(barrier, inc=1, device_id=(r, c), device_id_type=MESH)

    barrier = pltpu.get_barrier_semaphore()

    @pl.when(jnp.logical_not(diagonal))
    def _():
        for f in range(2):
            signal(2 * b + f, a)
            signal(2 * b + f, b)
        signal(2 * a + e, a)
        pl.semaphore_wait(barrier, 5)

    @pl.when(diagonal)
    def _():
        signal(2 * a + 1 - e, a)
        for s in range(1, n_col):
            other = lax.rem(a + s, n_col)
            if via_source:
                signal(2 * a + e, other)
                signal(2 * other, a)
                signal(2 * other + 1, a)
            else:
                signal(2 * other, a)
                signal(2 * other + 1, a)
                signal(2 * a + e, other)
        pl.semaphore_wait(barrier, 3 * (n_col - 1) + 1)

    def direct(k, f):
        return pltpu.make_async_remote_copy(
            src_ref=piece(k, f), dst_ref=land(e, k), send_sem=send_sem.at[f, k],
            recv_sem=recv_sem.at[e, k], device_id=(2 * b + f, a), device_id_type=MESH)

    def first_hop(k, f):
        if via_source:
            slot, place = (b, f, k), (2 * a + e, a)
        else:
            slot, place = (a, e, k), (2 * b + f, b)
        return pltpu.make_async_remote_copy(
            src_ref=piece(k, f), dst_ref=stage_ref.at[slot], send_sem=send_sem.at[f, k],
            recv_sem=stage_sem.at[slot], device_id=place, device_id_type=MESH)

    def second_hop(k, other, bit):
        if via_source:
            core, place = e, (2 * other + bit, a)
        else:
            core, place = bit, (2 * a + e, other)
        return pltpu.make_async_remote_copy(
            src_ref=stage_ref.at[other, bit, k], dst_ref=land(core, k),
            send_sem=pass_sem.at[other, bit, k], recv_sem=recv_sem.at[core, k],
            device_id=place, device_id_type=MESH)

    def own(k):
        return pltpu.make_async_copy(piece(k, e), land(e, k), own_sem.at[k])

    order = list(range(CHUNKS))

    @pl.when(jnp.logical_not(diagonal))
    def _():
        for k in order:
            for f in range(2):
                through = relayed(a, b, k)

                @pl.when(through)
                def _():
                    first_hop(k, f).start()

                @pl.when(jnp.logical_not(through))
                def _():
                    direct(k, f).start()

        for k in range(CHUNKS):
            for f in range(2):
                direct(k, f).wait_send()
                pltpu.make_async_remote_copy(
                    src_ref=land(f, k), dst_ref=land(f, k), send_sem=send_sem.at[f, k],
                    recv_sem=recv_sem.at[f, k], device_id=(2 * b + f, a),
                    device_id_type=MESH).wait_recv()

    def cross(k):
        return pltpu.make_async_remote_copy(
            src_ref=piece(k, 1 - e), dst_ref=land(e, k), send_sem=send_sem.at[0, k],
            recv_sem=recv_sem.at[e, k], device_id=(2 * a + 1 - e, a), device_id_type=MESH)

    def crossed(k):
        return pltpu.make_async_remote_copy(
            src_ref=land(1 - e, k), dst_ref=land(1 - e, k), send_sem=send_sem.at[0, k],
            recv_sem=recv_sem.at[1 - e, k], device_id=(2 * a + 1 - e, a), device_id_type=MESH)

    @pl.when(diagonal)
    def _():
        for k in range(CHUNKS):
            cross(k).start()
            own(k).start()

        def hops(act):
            for k in order:
                for s in range(1, n_col):
                    other = lax.rem(a + s, n_col)
                    source, target = (a, other) if via_source else (other, a)
                    for bit in range(2):
                        @pl.when(relayed(source, target, k))
                        def _():
                            act(second_hop(k, other, bit), k, other, bit)

        def forward(copy, k, other, bit):
            pltpu.make_async_remote_copy(
                src_ref=stage_ref.at[other, bit, k], dst_ref=stage_ref.at[other, bit, k],
                send_sem=pass_sem.at[other, bit, k], recv_sem=stage_sem.at[other, bit, k],
                device_id=(2 * a + 1 - e, a), device_id_type=MESH).wait_recv()
            copy.start()

        hops(forward)
        hops(lambda copy, k, other, bit: copy.wait_send())
        for k in range(CHUNKS):
            cross(k).wait_send()
            crossed(k).wait_recv()
            own(k).wait()


def exchange(mine, via_source=False):
    half, _, ch = mine.shape
    n_col = lax.axis_size("col")
    anywhere = pl.BlockSpec(memory_space=pl.ANY)
    out, _ = pl.pallas_call(
        functools.partial(exchange_kernel, via_source, n_col),
        out_shape=(jax.ShapeDtypeStruct((2, half, half, ch), BF16),
                   jax.ShapeDtypeStruct((n_col, 2, CHUNKS, half // CHUNKS, half, ch), BF16)),
        in_specs=[anywhere], out_specs=(anywhere, anywhere),
        scratch_shapes=[
            pltpu.SemaphoreType.DMA((2, CHUNKS)), pltpu.SemaphoreType.DMA((2, CHUNKS)),
            pltpu.SemaphoreType.DMA((n_col, 2, CHUNKS)), pltpu.SemaphoreType.DMA((n_col, 2, CHUNKS)),
            pltpu.SemaphoreType.DMA((CHUNKS,))],
        compiler_params=pltpu.CompilerParams(collective_id=0, has_side_effects=True),
    )(mine)
    return out


def mirror(mine):
    half, full, ch = mine.shape
    flipped = jnp.swapaxes(exchange(mine).reshape(full, half, ch), 0, 1)
    return ((mine.astype(F32) + flipped.astype(F32)) * 0.5).astype(BF16)


def halo(array, axis, dim, width):
    devices, length = lax.axis_size(axis), array.shape[dim]
    up = [(i, i + 1) for i in range(devices - 1)]
    down = [(j, i) for i, j in up]
    before = lax.ppermute(lax.slice_in_dim(array, length - width, length, axis=dim), axis, up)
    after = lax.ppermute(lax.slice_in_dim(array, 0, width, axis=dim), axis, down)
    return before, array, after


def per_device(contact_map, conv_weight, conv_bias):
    rows, cols, _ = contact_map.shape
    mirrored = mirror(contact_map)
    tall = jnp.concatenate(halo(mirrored, "row", 0, ROW_HALO), axis=0)
    pieces = halo(tall, "col", 1, COL_HALO)
    where = jnp.stack([
        lax.axis_index("row") * rows, lax.axis_index("col") * cols, lax.axis_size("row") * rows,
    ]).astype(jnp.int32)
    return trunk(pieces, where, conv_weight, conv_bias, rows, cols)


def solution(mesh):
    in_specs = (P("row", "col", None), P(), P())
    out_specs = P("row", "col", None)
    return jax.shard_map(
        per_device, mesh=mesh, in_specs=in_specs, out_specs=out_specs, check_vma=False
    )
```
